32 devices in a mesh: sky: 4 (over y, x), vel: 8 (over z, core).
Axes of the slice: x: 2, y: 2, z: 4, core: 2. Of those that a mesh axis runs over, the one named last changes fastest.
Arguments:
- psi_maps: float32 [4, 2048, 512], P(None, ('sky', 'vel')), may hold values from -6 to 6
- phi_maps: float32 [4, 2048, 512], P(None, ('sky', 'vel')), may hold values from 0.25 to 4
- psf_taps: float32 [9], replicated, may hold values from 0.1 to 1
- shifts: int32 [64, 4, 2], P('vel'), may hold values from -16 to 16, as said below
Outputs:
- likelihood: float32 [64, 2048, 512], P('vel', 'sky')
The draws below stay inside these ranges and needn't reach their ends.
Inputs may be any that keep to these rules, and one draw needn't show every extreme that they name: `shifts`: frame 0 has shift 0 in every trial.
All inputs are finite; a program needn't handle non-finite values.
Results may differ from the reference program's by a relative error of at most 0.0003.
Values sent between devices are 32-bit elements; how exact they have to be, the bound alone decides.
A program may use at most 128 MiB of HBM per device.

```python
import math
import jax
import jax.numpy as jnp
from jax import lax

FRAMES = 4
COLS = 512
KSIZE = 9
SHIFT = 16
NROWS = 2048
VELS = 64


def draw_shifts(key, part):
    values = jax.random.randint(key, (VELS, FRAMES, 2), -SHIFT, SHIFT + 1, dtype=jnp.int32)
    values = values.at[:, 0, :].set(0)
    values = values.at[0, FRAMES - 1, :].set(SHIFT)
    values = values.at[1, FRAMES - 1, :].set(-SHIFT)
    return values


def block_scale(rng, extent, cuts, smallest, largest):
    def one(dim, parts):
        steps = jax.random.uniform(jax.random.fold_in(jax.random.fold_in(rng, 6), dim), (parts,), jnp.float32, smallest / len(cuts), largest / len(cuts))
        return jnp.repeat(jnp.exp(steps), extent[dim] // parts).reshape((-1,) + (1,) * (len(extent) - dim - 1))

    gain = one(*cuts[0])
    for cut in cuts[1:]:
        gain = gain * one(*cut)
    return gain


def noise(rng, shape, spread, bound, shards=(), kind=jnp.bfloat16):
    loudness = block_scale(rng, shape, shards, -0.22, 0.18) if shards else 1.0
    array = jax.random.normal(rng, shape, jnp.float32) * spread * loudness
    return jnp.minimum(jnp.maximum(array, -bound), bound).astype(kind)


def setup_inputs(seed: int = 0) -> dict:
    splits = jax.random.split(jax.random.key(seed), 5)
    psi_maps = noise(splits[0], (FRAMES, NROWS, COLS), 1.0, 6.0, ((1, 32),), jnp.float32)
    phi_maps = jnp.clip(jnp.exp(math.log(4.0) - 2.7725887 * jax.random.uniform(splits[1], (FRAMES, NROWS, COLS), jnp.float32) ** block_scale(splits[1], (FRAMES, NROWS, COLS), ((1, 32),), -0.2, 0.2)), 0.25, 4.0)
    psf_taps = jnp.clip(jnp.exp(jax.random.uniform(splits[2], (KSIZE,), jnp.float32, math.log(0.1), math.log(1.0))), 0.1, 1.0)
    shifts = draw_shifts(jax.random.fold_in(splits[4], 71), 0)
    return dict(psi_maps=psi_maps, phi_maps=phi_maps, psf_taps=psf_taps, shifts=shifts)


def band_matrix(weights, width):
    row_index = lax.broadcasted_iota(jnp.int32, (width, width), 0)
    col_index = lax.broadcasted_iota(jnp.int32, (width, width), 1)
    offsets = row_index - col_index + weights.shape[0] // 2
    matrix = jnp.zeros((width, width), weights.dtype)
    for position in range(weights.shape[0]):
        matrix = matrix + jnp.where(offsets == position, weights[position], jnp.zeros((), weights.dtype))
    return matrix

def correlate(extended, weights, count):
    squared = weights * weights
    width = extended.shape[-1]
    along_psi = jnp.matmul(extended[0], band_matrix(weights, width), precision=lax.Precision.HIGHEST)
    along_phi = jnp.matmul(extended[1], band_matrix(squared, width), precision=lax.Precision.HIGHEST)
    blurred = jnp.stack([along_psi, along_phi])
    total = jnp.zeros(blurred.shape[:2] + (count, width), blurred.dtype)
    for position in range(weights.shape[0]):
        factor = jnp.stack([weights[position], squared[position]])
        total = total + factor[:, None, None, None] * blurred[:, :, position:position + count]
    return total

def reference(psi_maps, phi_maps, psf_taps, shifts):
    weights = psf_taps / jnp.sum(psf_taps)
    half = KSIZE // 2
    stacked = jnp.stack([psi_maps, phi_maps])
    padded = jnp.pad(stacked, ((0, 0), (0, 0), (half, half), (0, 0)))
    blurred = correlate(padded, weights, NROWS)
    reach = jnp.pad(blurred, ((0, 0), (0, 0), (SHIFT, SHIFT), (SHIFT, SHIFT)))
    anchor = jnp.zeros((), jnp.int32)

    def stack_trial(shift_rows):
        total = jnp.zeros((2, NROWS, COLS), reach.dtype)
        for frame in range(FRAMES):
            piece = lax.dynamic_slice(reach[:, frame], (anchor, (SHIFT + shift_rows[frame, 0]).astype(jnp.int32), (SHIFT + shift_rows[frame, 1]).astype(jnp.int32)), (2, NROWS, COLS))
            total = total + piece
        return total[0] / jnp.sqrt(total[1])
    return lax.map(stack_trial, shifts)
```

```python
import functools
import jax
import jax.numpy as jnp
from jax import lax
from jax.experimental import pallas as pl
from jax.experimental.pallas import tpu as pltpu
from jax.sharding import PartitionSpec as P

SHIFT = 16
EDGE = 24
LANES = 128
MESH = pl.DeviceIdType.MESH


def gather_kernel(
    vels, skies, taps_ref, psi_ref, phi_ref, out_ref,
    raw, along, top, bottom, band, weight,
    own_sem, recv_sem, right_sem, left_sem, pair_sem, top_recv, bottom_recv, top_send, bottom_send,
):
    frames, share, width = psi_ref.shape
    taps = taps_ref.shape[0]
    half = taps // 2
    maps = 2 * frames
    chips = vels // 2
    tiles = width // LANES
    both = 2 * share
    rows = vels * share
    sky = lax.axis_index("sky")
    vel = lax.axis_index("vel")
    chip = vel // 2
    core = vel % 2
    has_right = chip < chips - 1
    has_left = chip > 0
    has_next = sky < skies - 1
    has_prev = sky > 0

    own_psi = pltpu.make_async_copy(psi_ref, raw.at[vel, pl.ds(0, frames)], own_sem.at[0])
    own_phi = pltpu.make_async_copy(phi_ref, raw.at[vel, pl.ds(frames, frames)], own_sem.at[1])
    own_psi.start()
    own_phi.start()

    neighbours = (
        (has_right, (sky, vel + 2)),
        (has_left, (sky, vel - 2)),
        (has_next, (sky + 1, vel)),
        (has_prev, (sky - 1, vel)),
    )
    partner = (sky, vel + 1 - 2 * core)
    barrier = pltpu.get_barrier_semaphore()
    pl.semaphore_signal(barrier, inc=1, device_id=partner, device_id_type=MESH)
    for present, device in neighbours:

        @pl.when(present)
        def _(device=device):
            pl.semaphore_signal(barrier, inc=1, device_id=device, device_id_type=MESH)

    peers = 1
    for present, _ in neighbours:
        peers = peers + present.astype(jnp.int32)
    pl.semaphore_wait(barrier, peers)
    own_psi.wait()
    own_phi.wait()

    def line_copy(origin, m, to_right):
        chunk = 2 * origin + core
        return pltpu.make_async_remote_copy(
            src_ref=raw.at[chunk, m],
            dst_ref=raw.at[chunk, m],
            send_sem=(right_sem if to_right else left_sem).at[origin, m],
            recv_sem=recv_sem.at[chunk, m],
            device_id=(sky, vel + 2) if to_right else (sky, vel - 2),
            device_id_type=MESH,
        )

    def pair_copy(origin, m, side):
        chunk = 2 * origin + side
        return pltpu.make_async_remote_copy(
            src_ref=raw.at[chunk, m],
            dst_ref=raw.at[chunk, m],
            send_sem=pair_sem.at[origin, m],
            recv_sem=recv_sem.at[chunk, m],
            device_id=partner,
            device_id_type=MESH,
        )

    def top_copy(m):
        return pltpu.make_async_remote_copy(
            src_ref=raw.at[vels - 1, m, pl.ds(share - EDGE, EDGE)],
            dst_ref=top.at[m],
            send_sem=top_send.at[m],
            recv_sem=top_recv.at[m],
            device_id=(sky + 1, vel),
            device_id_type=MESH,
        )

    def bottom_copy(m):
        return pltpu.make_async_remote_copy(
            src_ref=raw.at[0, m, pl.ds(0, EDGE)],
            dst_ref=bottom.at[m],
            send_sem=bottom_send.at[m],
            recv_sem=bottom_recv.at[m],
            device_id=(sky - 1, vel),
            device_id_type=MESH,
        )

    def send_own(m, carry):
        @pl.when(has_right)
        def _():
            line_copy(chip, m, True).start()

        @pl.when(has_left)
        def _():
            line_copy(chip, m, False).start()

        pair_copy(chip, m, core).start()
        return carry

    lax.fori_loop(0, maps, send_own, 0)

    total = taps_ref[0]
    for i in range(1, taps):
        total = total + taps_ref[i]
    scale = 1.0 / jnp.full((8, LANES), total, jnp.float32)
    for i in range(taps):
        value = jnp.full((8, LANES), taps_ref[i], jnp.float32) * scale
        weight[0, i] = value
        weight[1, i] = value * value
    place = lax.broadcasted_iota(jnp.int32, (2 * LANES, LANES), 0)
    place = place - lax.broadcasted_iota(jnp.int32, (2 * LANES, LANES), 1)
    place = place - (LANES - SHIFT - half)
    for kind in range(2):
        matrix = jnp.zeros((2 * LANES, LANES), jnp.float32)
        for i in range(taps):
            value = jnp.broadcast_to(weight[kind, i][:1], (2 * LANES, LANES))
            matrix = jnp.where(place == i, value, matrix)
        coarse = matrix.astype(jnp.bfloat16)
        band[kind, 0] = coarse
        band[kind, 1] = (matrix - coarse.astype(jnp.float32)).astype(jnp.bfloat16)

    def blur_along(block, m, start):
        kind = m // frames
        count = block.shape[0]
        coarse = block.astype(jnp.bfloat16)
        fine = (block - coarse.astype(jnp.float32)).astype(jnp.bfloat16)
        for tile in range(tiles + 1):
            first, last = max(tile - 1, 0), min(tile + 1, tiles)
            columns = slice(first * LANES, last * LANES)
            offset = (first - tile + 1) * LANES
            depth = (last - first) * LANES
            high = band[kind, 0, offset : offset + depth]
            low = band[kind, 1, offset : offset + depth]
            value = jnp.dot(coarse[:, columns], high, preferred_element_type=jnp.float32)
            value += jnp.dot(fine[:, columns], high, preferred_element_type=jnp.float32)
            value += jnp.dot(coarse[:, columns], low, preferred_element_type=jnp.float32)
            if tile in (0, tiles):
                lane = lax.broadcasted_iota(jnp.int32, (count, LANES), 1)
                value = jnp.where(lane >= SHIFT if tile == 0 else lane < SHIFT, value, 0.0)
            along[m, tile, pl.ds(start, count)] = value

    def blur_across(m, start, count):
        kind = m // frames
        factors = [weight[kind, i] for i in range(taps)]

        def one_tile(tile, carry):
            for group in range(count // 8):
                base = start + 8 * group
                value = factors[0] * along[m, tile, pl.ds(base + 8 - half, 8)]
                for i in range(1, taps):
                    value += factors[i] * along[m, tile, pl.ds(base + 8 - half + i, 8)]
                out_ref[m, tile, pl.ds(pl.multiple_of(base, 8), 8)] = value
            return carry

        lax.fori_loop(0, tiles + 1, one_tile, 0)

    def arrive(distance, m):
        left = chip - distance
        right = chip + distance

        @pl.when((distance > 0) & (left >= 0))
        def _():
            line_copy(left, m, True).wait_recv()

            @pl.when(has_right)
            def _():
                line_copy(left, m, True).start()

            pair_copy(left, m, core).start()

        @pl.when((distance > 0) & (right < chips))
        def _():
            line_copy(right, m, False).wait_recv()

            @pl.when(has_left)
            def _():
                line_copy(right, m, False).start()

            pair_copy(right, m, core).start()

    def process(distance, m):
        def one_side(side, carry):
            origin = chip + (2 * side - 1) * distance

            @pl.when((origin >= 0) & (origin < chips) & ((side == 0) | (distance > 0)))
            def _():
                pair_copy(origin, m, 1 - core).wait_recv()

                @pl.when((origin == chips - 1) & has_next)
                def _():
                    top_copy(m).start()

                @pl.when((origin == 0) & has_prev)
                def _():
                    bottom_copy(m).start()

                def one_chunk(chunk, carry):
                    start = pl.multiple_of(EDGE + chunk * share, 8)
                    blur_along(raw[chunk, m], m, start)
                    return carry

                lax.fori_loop(2 * origin, 2 * origin + 2, one_chunk, 0)

                @pl.when(distance == 0)
                def _():
                    blur_across(m, SHIFT + origin * both + 8, both - 16)

                @pl.when(distance > 0)
                def _():
                    blur_across(m, SHIFT + origin * both + 8 - 16 * side, both)

            return carry

        lax.fori_loop(0, 2, one_side, 0)

    def step(index, carry):
        @pl.when(index < chips * maps)
        def _():
            arrive(index // maps, index % maps)

        @pl.when(index > 0)
        def _():
            process((index - 1) // maps, (index - 1) % maps)

        return carry

    lax.fori_loop(0, chips * maps + 1, step, 0)

    def finish(m, carry):
        @pl.when(has_prev)
        def _():
            pltpu.make_async_copy(top.at[m], top.at[m], top_recv.at[m]).wait()
            blur_along(top[m], m, 0)
            blur_across(m, 0, EDGE)

        @pl.when(jnp.logical_not(has_prev))
        def _():
            for tile in range(tiles + 1):
                along[m, tile, pl.ds(0, EDGE)] = jnp.zeros((EDGE, LANES), jnp.float32)
            blur_across(m, SHIFT, 8)
            for tile in range(tiles + 1):
                out_ref[m, tile, pl.ds(0, SHIFT)] = jnp.zeros((SHIFT, LANES), jnp.float32)

        @pl.when(has_next)
        def _():
            pltpu.make_async_copy(bottom.at[m], bottom.at[m], bottom_recv.at[m]).wait()
            blur_along(bottom[m], m, EDGE + rows)
            blur_across(m, SHIFT + rows - 8, EDGE)

        @pl.when(jnp.logical_not(has_next))
        def _():
            for tile in range(tiles + 1):
                along[m, tile, pl.ds(EDGE + rows, EDGE)] = jnp.zeros((EDGE, LANES), jnp.float32)
            blur_across(m, SHIFT + rows - 8, 8)
            for tile in range(tiles + 1):
                out_ref[m, tile, pl.ds(SHIFT + rows, SHIFT)] = jnp.zeros((SHIFT, LANES), jnp.float32)

        return carry

    lax.fori_loop(0, maps, finish, 0)

    def drain(index, carry):
        origin = index // maps
        m = index % maps

        @pl.when(has_right & (origin <= chip))
        def _():
            line_copy(origin, m, True).wait_send()

        @pl.when(has_left & (origin >= chip))
        def _():
            line_copy(origin, m, False).wait_send()

        pair_copy(origin, m, core).wait_send()

        @pl.when((origin == 0) & has_next)
        def _():
            top_copy(m).wait_send()

        @pl.when((origin == 0) & has_prev)
        def _():
            bottom_copy(m).wait_send()

        return carry

    lax.fori_loop(0, chips * maps, drain, 0)


def stack_kernel(shifts_ref, maps_ref, out_ref):
    frames = shifts_ref.shape[1]
    tiles = maps_ref.shape[1]
    trial = pl.program_id(0)
    lane = lax.broadcasted_iota(jnp.int32, (8, LANES), 1)
    down, turn, inside = [], [], []
    for frame in range(frames):
        offset = shifts_ref[trial, frame, 1] + SHIFT
        down.append(shifts_ref[trial, frame, 0] + SHIFT)
        turn.append(lax.rem(LANES - offset, LANES))
        inside.append(lane < LANES - offset)

    def one_group(group, carry):
        base = group * 8

        def stacked(kind):
            total = [None] * (tiles - 1)
            for frame in range(frames):
                m = kind * frames + frame
                rolled = [
                    pltpu.roll(maps_ref[m, tile, pl.ds(base + down[frame], 8)], turn[frame], 1)
                    for tile in range(tiles)
                ]
                for tile in range(tiles - 1):
                    piece = jnp.where(inside[frame], rolled[tile], rolled[tile + 1])
                    total[tile] = piece if frame == 0 else total[tile] + piece
            return total

        psi = stacked(0)
        phi = stacked(1)
        for tile in range(tiles - 1):
            out_ref[0, pl.ds(pl.multiple_of(base, 8), 8), tile * LANES : (tile + 1) * LANES] = (
                psi[tile] * lax.rsqrt(phi[tile])
            )
        return carry

    lax.fori_loop(0, out_ref.shape[1] // 8, one_group, 0, unroll=2)


def per_device(vels, skies, psi_maps, phi_maps, psf_taps, shifts):
    frames, share, width = psi_maps.shape
    maps = 2 * frames
    tiles = width // LANES
    rows = share * vels
    trials = shifts.shape[0]
    dma = pltpu.SemaphoreType.DMA
    blurred = pl.pallas_call(
        functools.partial(gather_kernel, vels, skies),
        out_shape=jax.ShapeDtypeStruct((maps, tiles + 1, rows + 2 * SHIFT, LANES), jnp.float32),
        in_specs=[
            pl.BlockSpec(memory_space=pltpu.SMEM),
            pl.BlockSpec(memory_space=pl.ANY),
            pl.BlockSpec(memory_space=pl.ANY),
        ],
        out_specs=pl.BlockSpec(memory_space=pltpu.VMEM),
        scratch_shapes=[
            pltpu.VMEM((vels, maps, share, width), jnp.float32),
            pltpu.VMEM((maps, tiles + 1, rows + 2 * EDGE, LANES), jnp.float32),
            pltpu.VMEM((maps, EDGE, width), jnp.float32),
            pltpu.VMEM((maps, EDGE, width), jnp.float32),
            pltpu.VMEM((2, 2, 2 * LANES, LANES), jnp.bfloat16),
            pltpu.VMEM((2, psf_taps.shape[0], 8, LANES), jnp.float32),
            dma((2,)),
            dma((vels, maps)),
            dma((vels // 2, maps)),
            dma((vels // 2, maps)),
            dma((vels // 2, maps)),
            dma((maps,)),
            dma((maps,)),
            dma((maps,)),
            dma((maps,)),
        ],
        compiler_params=pltpu.CompilerParams(
            collective_id=0, has_side_effects=True, vmem_limit_bytes=24 * 2**20
        ),
        name="gather",
    )(psf_taps, psi_maps, phi_maps)
    return pl.pallas_call(
        stack_kernel,
        grid=(trials,),
        out_shape=jax.ShapeDtypeStruct((trials, rows, width), jnp.float32),
        in_specs=[
            pl.BlockSpec(memory_space=pltpu.SMEM),
            pl.BlockSpec(memory_space=pltpu.VMEM),
        ],
        out_specs=pl.BlockSpec((1, rows, width), lambda t: (t, 0, 0)),
        compiler_params=pltpu.CompilerParams(vmem_limit_bytes=4 * 2**20),
        name="stack",
    )(shifts, blurred)


def solution(mesh):
    return jax.shard_map(
        functools.partial(per_device, mesh.shape["vel"], mesh.shape["sky"]),
        mesh=mesh,
        in_specs=(
            P(None, ("sky", "vel"), None),
            P(None, ("sky", "vel"), None),
            P(),
            P("vel", None, None),
        ),
        out_specs=P("vel", "sky", None),
        check_vma=False,
    )
```

```python
import functools
import jax
import jax.numpy as jnp
from jax import lax
from jax.experimental import pallas as pl
from jax.experimental.pallas import tpu as pltpu
from jax.sharding import PartitionSpec as P

SHIFT = 16
EDGE = 24
LANES = 128
MESH = pl.DeviceIdType.MESH


def gather_kernel(
    vels, skies, taps_ref, psi_ref, phi_ref, out_ref,
    raw, along, top, bottom, band, weight,
    own_sem, recv_sem, right_sem, left_sem, pair_sem, top_recv, bottom_recv, top_send, bottom_send,
):
    frames, share, width = psi_ref.shape
    taps = taps_ref.shape[0]
    half = taps // 2
    maps = 2 * frames
    chips = vels // 2
    tiles = width // LANES
    both = 2 * share
    rows = vels * share
    sky = lax.axis_index("sky")
    vel = lax.axis_index("vel")
    chip = vel // 2
    core = vel % 2
    has_right = chip < chips - 1
    has_left = chip > 0
    has_next = sky < skies - 1
    has_prev = sky > 0

    own_psi = pltpu.make_async_copy(psi_ref, raw.at[vel, pl.ds(0, frames)], own_sem.at[0])
    own_phi = pltpu.make_async_copy(phi_ref, raw.at[vel, pl.ds(frames, frames)], own_sem.at[1])
    own_psi.start()
    own_phi.start()

    neighbours = (
        (has_right, (sky, vel + 2)),
        (has_left, (sky, vel - 2)),
        (has_next, (sky + 1, vel)),
        (has_prev, (sky - 1, vel)),
    )
    partner = (sky, vel + 1 - 2 * core)
    barrier = pltpu.get_barrier_semaphore()
    pl.semaphore_signal(barrier, inc=1, device_id=partner, device_id_type=MESH)
    for present, device in neighbours:

        @pl.when(present)
        def _(device=device):
            pl.semaphore_signal(barrier, inc=1, device_id=device, device_id_type=MESH)

    peers = 1
    for present, _ in neighbours:
        peers = peers + present.astype(jnp.int32)
    pl.semaphore_wait(barrier, peers)
    own_psi.wait()
    own_phi.wait()

    def line_copy(origin, m, to_right):
        chunk = 2 * origin + core
        return pltpu.make_async_remote_copy(
            src_ref=raw.at[chunk, m],
            dst_ref=raw.at[chunk, m],
            send_sem=(right_sem if to_right else left_sem).at[origin, m],
            recv_sem=recv_sem.at[chunk, m],
            device_id=(sky, vel + 2) if to_right else (sky, vel - 2),
            device_id_type=MESH,
        )

    def pair_copy(origin, m, side):
        chunk = 2 * origin + side
        return pltpu.make_async_remote_copy(
            src_ref=raw.at[chunk, m],
            dst_ref=raw.at[chunk, m],
            send_sem=pair_sem.at[origin, m],
            recv_sem=recv_sem.at[chunk, m],
            device_id=partner,
            device_id_type=MESH,
        )

    def top_copy(m):
        return pltpu.make_async_remote_copy(
            src_ref=raw.at[vels - 1, m, pl.ds(share - EDGE, EDGE)],
            dst_ref=top.at[m],
            send_sem=top_send.at[m],
            recv_sem=top_recv.at[m],
            device_id=(sky + 1, vel),
            device_id_type=MESH,
        )

    def bottom_copy(m):
        return pltpu.make_async_remote_copy(
            src_ref=raw.at[0, m, pl.ds(0, EDGE)],
            dst_ref=bottom.at[m],
            send_sem=bottom_send.at[m],
            recv_sem=bottom_recv.at[m],
            device_id=(sky - 1, vel),
            device_id_type=MESH,
        )

    def send_own(m, carry):
        @pl.when(has_right)
        def _():
            line_copy(chip, m, True).start()

        @pl.when(has_left)
        def _():
            line_copy(chip, m, False).start()

        pair_copy(chip, m, core).start()
        return carry

    lax.fori_loop(0, maps, send_own, 0)

    total = taps_ref[0]
    for i in range(1, taps):
        total = total + taps_ref[i]
    scale = 1.0 / jnp.full((8, LANES), total, jnp.float32)
    for i in range(taps):
        value = jnp.full((8, LANES), taps_ref[i], jnp.float32) * scale
        weight[0, i] = value
        weight[1, i] = value * value
    place = lax.broadcasted_iota(jnp.int32, (3 * LANES, LANES), 0)
    place = place - lax.broadcasted_iota(jnp.int32, (3 * LANES, LANES), 1)
    for lead in range(2):
        spot = place - (LANES - SHIFT * lead - half)
        for kind in range(2):
            matrix = jnp.zeros((3 * LANES, LANES), jnp.float32)
            for i in range(taps):
                value = jnp.broadcast_to(weight[kind, i][:1], (3 * LANES, LANES))
                matrix = jnp.where(spot == i, value, matrix)
            coarse = matrix.astype(jnp.bfloat16)
            band[lead, kind, 0] = coarse
            band[lead, kind, 1] = (matrix - coarse.astype(jnp.float32)).astype(jnp.bfloat16)

    def blur_along(block, m, start):
        kind = m // frames
        count = block.shape[0]
        coarse = block.astype(jnp.bfloat16)
        fine = (block - coarse.astype(jnp.float32)).astype(jnp.bfloat16)

        def place_tiles(lead):
            for tile in range(tiles + lead):
                first, last = max(tile - 1, 0), min(tile + 2 - lead, tiles)
                columns = slice(first * LANES, last * LANES)
                offset = (first - tile + 1) * LANES
                depth = (last - first) * LANES
                high = band[lead, kind, 0, offset : offset + depth]
                low = band[lead, kind, 1, offset : offset + depth]
                value = jnp.dot(coarse[:, columns], high, preferred_element_type=jnp.float32)
                value += jnp.dot(fine[:, columns], high, preferred_element_type=jnp.float32)
                value += jnp.dot(coarse[:, columns], low, preferred_element_type=jnp.float32)
                if lead and tile in (0, tiles):
                    lane = lax.broadcasted_iota(jnp.int32, (count, LANES), 1)
                    value = jnp.where(lane >= SHIFT if tile == 0 else lane < SHIFT, value, 0.0)
                along[m, tile, pl.ds(start, count)] = value

        @pl.when(m % frames == 0)
        def _():
            place_tiles(0)

        @pl.when(m % frames > 0)
        def _():
            place_tiles(1)

    def blur_across(m, start, count):
        kind = m // frames
        factors = [weight[kind, i] for i in range(taps)]

        def one_tile(tile, carry):
            for group in range(count // 8):
                base = start + 8 * group
                value = factors[0] * along[m, tile, pl.ds(base + 8 - half, 8)]
                for i in range(1, taps):
                    value += factors[i] * along[m, tile, pl.ds(base + 8 - half + i, 8)]
                out_ref[m, tile, pl.ds(pl.multiple_of(base, 8), 8)] = value
            return carry

        lax.fori_loop(0, tiles + jnp.minimum(m % frames, 1), one_tile, 0)

    def arrive(distance, m):
        left = chip - distance
        right = chip + distance

        @pl.when((distance > 0) & (left >= 0))
        def _():
            line_copy(left, m, True).wait_recv()

            @pl.when(has_right)
            def _():
                line_copy(left, m, True).start()

            pair_copy(left, m, core).start()

        @pl.when((distance > 0) & (right < chips))
        def _():
            line_copy(right, m, False).wait_recv()

            @pl.when(has_left)
            def _():
                line_copy(right, m, False).start()

            pair_copy(right, m, core).start()

    def process(distance, m):
        def one_side(side, carry):
            origin = chip + (2 * side - 1) * distance

            @pl.when((origin >= 0) & (origin < chips) & ((side == 0) | (distance > 0)))
            def _():
                pair_copy(origin, m, 1 - core).wait_recv()

                @pl.when((origin == chips - 1) & has_next)
                def _():
                    top_copy(m).start()

                @pl.when((origin == 0) & has_prev)
                def _():
                    bottom_copy(m).start()

                def one_chunk(chunk, carry):
                    start = pl.multiple_of(EDGE + chunk * share, 8)
                    blur_along(raw[chunk, m], m, start)
                    return carry

                lax.fori_loop(2 * origin, 2 * origin + 2, one_chunk, 0)

                @pl.when(distance == 0)
                def _():
                    blur_across(m, SHIFT + origin * both + 8, both - 16)

                @pl.when(distance > 0)
                def _():
                    blur_across(m, SHIFT + origin * both + 8 - 16 * side, both)

            return carry

        lax.fori_loop(0, 2, one_side, 0)

    def step(index, carry):
        @pl.when(index < chips * maps)
        def _():
            arrive(index // maps, index % maps)

        @pl.when(index > 0)
        def _():
            process((index - 1) // maps, (index - 1) % maps)

        return carry

    lax.fori_loop(0, chips * maps + 1, step, 0)

    def finish(m, carry):
        @pl.when(has_prev)
        def _():
            pltpu.make_async_copy(top.at[m], top.at[m], top_recv.at[m]).wait()
            blur_along(top[m], m, 0)
            blur_across(m, 0, EDGE)

        @pl.when(jnp.logical_not(has_prev))
        def _():
            for tile in range(tiles + 1):
                along[m, tile, pl.ds(0, EDGE)] = jnp.zeros((EDGE, LANES), jnp.float32)
            blur_across(m, SHIFT, 8)
            for tile in range(tiles + 1):
                out_ref[m, tile, pl.ds(0, SHIFT)] = jnp.zeros((SHIFT, LANES), jnp.float32)

        @pl.when(has_next)
        def _():
            pltpu.make_async_copy(bottom.at[m], bottom.at[m], bottom_recv.at[m]).wait()
            blur_along(bottom[m], m, EDGE + rows)
            blur_across(m, SHIFT + rows - 8, EDGE)

        @pl.when(jnp.logical_not(has_next))
        def _():
            for tile in range(tiles + 1):
                along[m, tile, pl.ds(EDGE + rows, EDGE)] = jnp.zeros((EDGE, LANES), jnp.float32)
            blur_across(m, SHIFT + rows - 8, 8)
            for tile in range(tiles + 1):
                out_ref[m, tile, pl.ds(SHIFT + rows, SHIFT)] = jnp.zeros((SHIFT, LANES), jnp.float32)

        return carry

    lax.fori_loop(0, maps, finish, 0)

    def drain(index, carry):
        origin = index // maps
        m = index % maps

        @pl.when(has_right & (origin <= chip))
        def _():
            line_copy(origin, m, True).wait_send()

        @pl.when(has_left & (origin >= chip))
        def _():
            line_copy(origin, m, False).wait_send()

        pair_copy(origin, m, core).wait_send()

        @pl.when((origin == 0) & has_next)
        def _():
            top_copy(m).wait_send()

        @pl.when((origin == 0) & has_prev)
        def _():
            bottom_copy(m).wait_send()

        return carry

    lax.fori_loop(0, chips * maps, drain, 0)


def stack_kernel(shifts_ref, maps_ref, out_ref):
    frames = shifts_ref.shape[1]
    tiles = maps_ref.shape[1]
    trial = pl.program_id(0)
    lane = lax.broadcasted_iota(jnp.int32, (8, LANES), 1)
    down, turn, inside = [], [], []
    for frame in range(1, frames):
        offset = shifts_ref[trial, frame, 1] + SHIFT
        down.append(shifts_ref[trial, frame, 0] + SHIFT)
        turn.append(lax.rem(LANES - offset, LANES))
        inside.append(lane >= offset)

    def one_group(group, carry):
        base = group * 8

        def stacked(kind):
            total = [
                maps_ref[kind * frames, tile, pl.ds(pl.multiple_of(base + SHIFT, 8), 8)]
                for tile in range(tiles - 1)
            ]
            for step in range(frames - 1):
                m = kind * frames + step + 1
                pieces = [maps_ref[m, tile, pl.ds(base + down[step], 8)] for tile in range(tiles)]
                for tile in range(tiles - 1):
                    joined = jnp.where(inside[step], pieces[tile], pieces[tile + 1])
                    total[tile] = total[tile] + pltpu.roll(joined, turn[step], 1)
            return total

        psi = stacked(0)
        phi = stacked(1)
        for tile in range(tiles - 1):
            out_ref[0, pl.ds(pl.multiple_of(base, 8), 8), tile * LANES : (tile + 1) * LANES] = (
                psi[tile] * lax.rsqrt(phi[tile])
            )
        return carry

    lax.fori_loop(0, out_ref.shape[1] // 8, one_group, 0, unroll=8)


def per_device(vels, skies, psi_maps, phi_maps, psf_taps, shifts):
    frames, share, width = psi_maps.shape
    maps = 2 * frames
    tiles = width // LANES
    rows = share * vels
    trials = shifts.shape[0]
    dma = pltpu.SemaphoreType.DMA
    blurred = pl.pallas_call(
        functools.partial(gather_kernel, vels, skies),
        out_shape=jax.ShapeDtypeStruct((maps, tiles + 1, rows + 2 * SHIFT, LANES), jnp.float32),
        in_specs=[
            pl.BlockSpec(memory_space=pltpu.SMEM),
            pl.BlockSpec(memory_space=pl.ANY),
            pl.BlockSpec(memory_space=pl.ANY),
        ],
        out_specs=pl.BlockSpec(memory_space=pltpu.VMEM),
        scratch_shapes=[
            pltpu.VMEM((vels, maps, share, width), jnp.float32),
            pltpu.VMEM((maps, tiles + 1, rows + 2 * EDGE, LANES), jnp.float32),
            pltpu.VMEM((maps, EDGE, width), jnp.float32),
            pltpu.VMEM((maps, EDGE, width), jnp.float32),
            pltpu.VMEM((2, 2, 2, 3 * LANES, LANES), jnp.bfloat16),
            pltpu.VMEM((2, psf_taps.shape[0], 8, LANES), jnp.float32),
            dma((2,)),
            dma((vels, maps)),
            dma((vels // 2, maps)),
            dma((vels // 2, maps)),
            dma((vels // 2, maps)),
            dma((maps,)),
            dma((maps,)),
            dma((maps,)),
            dma((maps,)),
        ],
        compiler_params=pltpu.CompilerParams(
            collective_id=0, has_side_effects=True, vmem_limit_bytes=24 * 2**20
        ),
        name="gather",
    )(psf_taps, psi_maps, phi_maps)
    return pl.pallas_call(
        stack_kernel,
        grid=(trials,),
        out_shape=jax.ShapeDtypeStruct((trials, rows, width), jnp.float32),
        in_specs=[
            pl.BlockSpec(memory_space=pltpu.SMEM),
            pl.BlockSpec(memory_space=pltpu.VMEM),
        ],
        out_specs=pl.BlockSpec((1, rows, width), lambda t: (t, 0, 0)),
        compiler_params=pltpu.CompilerParams(vmem_limit_bytes=4 * 2**20),
        name="stack",
    )(shifts, blurred)


def solution(mesh):
    return jax.shard_map(
        functools.partial(per_device, mesh.shape["vel"], mesh.shape["sky"]),
        mesh=mesh,
        in_specs=(
            P(None, ("sky", "vel"), None),
            P(None, ("sky", "vel"), None),
            P(),
            P("vel", None, None),
        ),
        out_specs=P("vel", "sky", None),
        check_vma=False,
    )
```

```python
import functools
import jax
import jax.numpy as jnp
from jax import lax
from jax.experimental import pallas as pl
from jax.experimental.pallas import tpu as pltpu
from jax.sharding import PartitionSpec as P

SHIFT = 16
EDGE = 24
LANES = 128
MESH = pl.DeviceIdType.MESH


def stack_rows(shifts_ref, maps_ref, out_ref, trial, first, count, shift, unroll):
    frames = shifts_ref.shape[1]
    tiles = maps_ref.shape[1]
    lane = lax.broadcasted_iota(jnp.int32, (8, LANES), 1)
    down, turn, inside = [], [], []
    for frame in range(1, frames):
        offset = shifts_ref[trial, frame, 1] + SHIFT
        down.append(shifts_ref[trial, frame, 0] + SHIFT)
        turn.append(lax.rem(LANES - offset, LANES))
        inside.append(lane >= offset)

    def one_group(group, carry):
        base = first + group * 8

        def stacked(kind):
            total = [
                maps_ref[kind * frames, tile, pl.ds(pl.multiple_of(base + SHIFT, 8), 8)]
                for tile in range(tiles - 1)
            ]
            for step in range(frames - 1):
                m = kind * frames + step + 1
                pieces = [maps_ref[m, tile, pl.ds(base + down[step], 8)] for tile in range(tiles)]
                for tile in range(tiles - 1):
                    joined = jnp.where(inside[step], pieces[tile], pieces[tile + 1])
                    total[tile] = total[tile] + pltpu.roll(joined, turn[step], 1)
            return total

        psi = stacked(0)
        phi = stacked(1)
        for tile in range(tiles - 1):
            out_ref[
                trial, pl.ds(pl.multiple_of(base - shift, 8), 8), tile * LANES : (tile + 1) * LANES
            ] = psi[tile] * lax.rsqrt(phi[tile])
        return carry

    lax.fori_loop(0, count // 8, one_group, 0, unroll=unroll)


def stack_kernel(vels, shifts_ref, maps_ref, done_ref, out_ref, near, far, sems):
    trials, rows, _ = done_ref.shape
    both = 2 * (rows // vels)
    chip = lax.axis_index("vel") // 2
    low = (chip < vels // 4).astype(jnp.int32)
    middle = rows - both - 2 * EDGE
    middle_row = pl.multiple_of(EDGE + (1 - low) * both, 8)
    near_row = pl.multiple_of((1 - low) * (rows - EDGE), 8)
    far_row = pl.multiple_of(low * (rows - both - EDGE), 8)

    def middle_copy(trial):
        part = pl.ds(middle_row, middle)
        return pltpu.make_async_copy(done_ref.at[trial, part], out_ref.at[trial, part], sems.at[0, trial])

    def near_copy(trial):
        return pltpu.make_async_copy(
            near.at[trial], out_ref.at[trial, pl.ds(near_row, EDGE)], sems.at[1, trial]
        )

    def far_copy(trial):
        return pltpu.make_async_copy(
            far.at[trial], out_ref.at[trial, pl.ds(far_row, both + EDGE)], sems.at[2, trial]
        )

    def begin(trial, carry):
        middle_copy(trial).start()
        return carry

    lax.fori_loop(0, trials, begin, 0)

    def compute(trial, carry):
        stack_rows(shifts_ref, maps_ref, near, trial, near_row, EDGE, near_row, 3)
        near_copy(trial).start()
        stack_rows(shifts_ref, maps_ref, far, trial, far_row, both + EDGE, far_row, True)
        far_copy(trial).start()
        return carry

    lax.fori_loop(0, trials, compute, 0)

    def finish(trial, carry):
        middle_copy(trial).wait()
        near_copy(trial).wait()
        far_copy(trial).wait()
        return carry

    lax.fori_loop(0, trials, finish, 0)


def gather_kernel(
    vels, skies, taps_ref, shifts_ref, psi_ref, phi_ref, out_ref, done_ref,
    raw, along, top, bottom, band, weight,
    own_sem, recv_sem, right_sem, left_sem, pair_sem, top_recv, bottom_recv, top_send, bottom_send,
):
    frames, share, width = psi_ref.shape
    taps = taps_ref.shape[0]
    half = taps // 2
    maps = 2 * frames
    chips = vels // 2
    tiles = width // LANES
    both = 2 * share
    rows = vels * share
    sky = lax.axis_index("sky")
    vel = lax.axis_index("vel")
    chip = vel // 2
    core = vel % 2
    has_right = chip < chips - 1
    has_left = chip > 0
    has_next = sky < skies - 1
    has_prev = sky > 0

    own_psi = pltpu.make_async_copy(psi_ref, raw.at[vel, pl.ds(0, frames)], own_sem.at[0])
    own_phi = pltpu.make_async_copy(phi_ref, raw.at[vel, pl.ds(frames, frames)], own_sem.at[1])
    own_psi.start()
    own_phi.start()

    neighbours = (
        (has_right, (sky, vel + 2)),
        (has_left, (sky, vel - 2)),
        (has_next, (sky + 1, vel)),
        (has_prev, (sky - 1, vel)),
    )
    partner = (sky, vel + 1 - 2 * core)
    barrier = pltpu.get_barrier_semaphore()
    pl.semaphore_signal(barrier, inc=1, device_id=partner, device_id_type=MESH)
    for present, device in neighbours:

        @pl.when(present)
        def _(device=device):
            pl.semaphore_signal(barrier, inc=1, device_id=device, device_id_type=MESH)

    peers = 1
    for present, _ in neighbours:
        peers = peers + present.astype(jnp.int32)
    pl.semaphore_wait(barrier, peers)
    own_psi.wait()
    own_phi.wait()

    def line_copy(origin, m, to_right):
        chunk = 2 * origin + core
        return pltpu.make_async_remote_copy(
            src_ref=raw.at[chunk, m],
            dst_ref=raw.at[chunk, m],
            send_sem=(right_sem if to_right else left_sem).at[origin, m],
            recv_sem=recv_sem.at[chunk, m],
            device_id=(sky, vel + 2) if to_right else (sky, vel - 2),
            device_id_type=MESH,
        )

    def pair_copy(origin, m, side):
        chunk = 2 * origin + side
        return pltpu.make_async_remote_copy(
            src_ref=raw.at[chunk, m],
            dst_ref=raw.at[chunk, m],
            send_sem=pair_sem.at[origin, m],
            recv_sem=recv_sem.at[chunk, m],
            device_id=partner,
            device_id_type=MESH,
        )

    def top_copy(m):
        return pltpu.make_async_remote_copy(
            src_ref=raw.at[vels - 1, m, pl.ds(share - EDGE, EDGE)],
            dst_ref=top.at[m],
            send_sem=top_send.at[m],
            recv_sem=top_recv.at[m],
            device_id=(sky + 1, vel),
            device_id_type=MESH,
        )

    def bottom_copy(m):
        return pltpu.make_async_remote_copy(
            src_ref=raw.at[0, m, pl.ds(0, EDGE)],
            dst_ref=bottom.at[m],
            send_sem=bottom_send.at[m],
            recv_sem=bottom_recv.at[m],
            device_id=(sky - 1, vel),
            device_id_type=MESH,
        )

    def send_own(m, carry):
        @pl.when(has_right)
        def _():
            line_copy(chip, m, True).start()

        @pl.when(has_left)
        def _():
            line_copy(chip, m, False).start()

        pair_copy(chip, m, core).start()
        return carry

    lax.fori_loop(0, maps, send_own, 0)

    total = taps_ref[0]
    for i in range(1, taps):
        total = total + taps_ref[i]
    scale = 1.0 / jnp.full((8, LANES), total, jnp.float32)
    for i in range(taps):
        value = jnp.full((8, LANES), taps_ref[i], jnp.float32) * scale
        weight[0, i] = value
        weight[1, i] = value * value
    place = lax.broadcasted_iota(jnp.int32, (3 * LANES, LANES), 0)
    place = place - lax.broadcasted_iota(jnp.int32, (3 * LANES, LANES), 1)
    for lead in range(2):
        spot = place - (LANES - SHIFT * lead - half)
        for kind in range(2):
            matrix = jnp.zeros((3 * LANES, LANES), jnp.float32)
            for i in range(taps):
                value = jnp.broadcast_to(weight[kind, i][:1], (3 * LANES, LANES))
                matrix = jnp.where(spot == i, value, matrix)
            coarse = matrix.astype(jnp.bfloat16)
            band[lead, kind, 0] = coarse
            band[lead, kind, 1] = (matrix - coarse.astype(jnp.float32)).astype(jnp.bfloat16)

    def blur_along(block, m, start):
        kind = m // frames
        count = block.shape[0]
        coarse = block.astype(jnp.bfloat16)
        fine = (block - coarse.astype(jnp.float32)).astype(jnp.bfloat16)

        def place_tiles(lead):
            for tile in range(tiles + lead):
                first, last = max(tile - 1, 0), min(tile + 2 - lead, tiles)
                columns = slice(first * LANES, last * LANES)
                offset = (first - tile + 1) * LANES
                depth = (last - first) * LANES
                high = band[lead, kind, 0, offset : offset + depth]
                low = band[lead, kind, 1, offset : offset + depth]
                value = jnp.dot(coarse[:, columns], high, preferred_element_type=jnp.float32)
                value += jnp.dot(fine[:, columns], high, preferred_element_type=jnp.float32)
                value += jnp.dot(coarse[:, columns], low, preferred_element_type=jnp.float32)
                if lead and tile in (0, tiles):
                    lane = lax.broadcasted_iota(jnp.int32, (count, LANES), 1)
                    value = jnp.where(lane >= SHIFT if tile == 0 else lane < SHIFT, value, 0.0)
                along[m, tile, pl.ds(start, count)] = value

        @pl.when(m % frames == 0)
        def _():
            place_tiles(0)

        @pl.when(m % frames > 0)
        def _():
            place_tiles(1)

    def blur_across(m, start, count):
        kind = m // frames
        factors = [weight[kind, i] for i in range(taps)]

        def one_tile(tile, carry):
            for group in range(count // 8):
                base = start + 8 * group
                value = factors[0] * along[m, tile, pl.ds(base + 8 - half, 8)]
                for i in range(1, taps):
                    value += factors[i] * along[m, tile, pl.ds(base + 8 - half + i, 8)]
                out_ref[m, tile, pl.ds(pl.multiple_of(base, 8), 8)] = value
            return carry

        lax.fori_loop(0, tiles + jnp.minimum(m % frames, 1), one_tile, 0)

    def arrive(distance, m):
        left = chip - distance
        right = chip + distance

        @pl.when((distance > 0) & (left >= 0))
        def _():
            line_copy(left, m, True).wait_recv()

            @pl.when(has_right)
            def _():
                line_copy(left, m, True).start()

            pair_copy(left, m, core).start()

        @pl.when((distance > 0) & (right < chips))
        def _():
            line_copy(right, m, False).wait_recv()

            @pl.when(has_left)
            def _():
                line_copy(right, m, False).start()

            pair_copy(right, m, core).start()

    def process(distance, m):
        def one_side(side, carry):
            origin = chip + (2 * side - 1) * distance

            @pl.when((origin >= 0) & (origin < chips) & ((side == 0) | (distance > 0)))
            def _():
                pair_copy(origin, m, 1 - core).wait_recv()

                @pl.when((origin == chips - 1) & has_next)
                def _():
                    top_copy(m).start()

                @pl.when((origin == 0) & has_prev)
                def _():
                    bottom_copy(m).start()

                def one_chunk(chunk, carry):
                    start = pl.multiple_of(EDGE + chunk * share, 8)
                    blur_along(raw[chunk, m], m, start)
                    return carry

                lax.fori_loop(2 * origin, 2 * origin + 2, one_chunk, 0)

                @pl.when(distance == 0)
                def _():
                    blur_across(m, SHIFT + origin * both + 8, both - 16)

                @pl.when(distance > 0)
                def _():
                    blur_across(m, SHIFT + origin * both + 8 - 16 * side, both)

            return carry

        lax.fori_loop(0, 2, one_side, 0)

    lead = jnp.where(chip < chips // 2, chips - 1, 0)

    def stack_side(distance, trial):
        def one_side(side, carry):
            origin = chip + (2 * side - 1) * distance
            wanted = (origin >= 0) & (origin < chips) & (origin != lead)

            @pl.when(wanted & (distance == 0) & (side == 0))
            def _():
                first = origin * both + EDGE
                stack_rows(shifts_ref, out_ref, done_ref, trial, first, both - 2 * EDGE, 0, 2)

            @pl.when(wanted & (distance > 0))
            def _():
                first = origin * both + EDGE - 2 * EDGE * side
                stack_rows(shifts_ref, out_ref, done_ref, trial, first, both, 0, 8)

            return carry

        lax.fori_loop(0, 2, one_side, 0)

    def step(index, carry):
        @pl.when(index < chips * maps)
        def _():
            arrive(index // maps, index % maps)

        @pl.when(index > 0)
        def _():
            process((index - 1) // maps, (index - 1) % maps)

        @pl.when(index > maps)
        def _():
            for block in range(0, shifts_ref.shape[0], maps):
                trial = (index - 1) % maps + block

                @pl.when(trial < shifts_ref.shape[0])
                def _(trial=trial):
                    stack_side((index - 1) // maps - 1, trial)

        return carry

    lax.fori_loop(0, chips * maps + 1, step, 0)

    def finish(m, carry):
        @pl.when(has_prev)
        def _():
            pltpu.make_async_copy(top.at[m], top.at[m], top_recv.at[m]).wait()
            blur_along(top[m], m, 0)
            blur_across(m, 0, EDGE)

        @pl.when(jnp.logical_not(has_prev))
        def _():
            for tile in range(tiles + 1):
                along[m, tile, pl.ds(0, EDGE)] = jnp.zeros((EDGE, LANES), jnp.float32)
            blur_across(m, SHIFT, 8)
            for tile in range(tiles + 1):
                out_ref[m, tile, pl.ds(0, SHIFT)] = jnp.zeros((SHIFT, LANES), jnp.float32)

        @pl.when(has_next)
        def _():
            pltpu.make_async_copy(bottom.at[m], bottom.at[m], bottom_recv.at[m]).wait()
            blur_along(bottom[m], m, EDGE + rows)
            blur_across(m, SHIFT + rows - 8, EDGE)

        @pl.when(jnp.logical_not(has_next))
        def _():
            for tile in range(tiles + 1):
                along[m, tile, pl.ds(EDGE + rows, EDGE)] = jnp.zeros((EDGE, LANES), jnp.float32)
            blur_across(m, SHIFT + rows - 8, 8)
            for tile in range(tiles + 1):
                out_ref[m, tile, pl.ds(SHIFT + rows, SHIFT)] = jnp.zeros((SHIFT, LANES), jnp.float32)

        return carry

    lax.fori_loop(0, maps, finish, 0)

    def drain(index, carry):
        origin = index // maps
        m = index % maps

        @pl.when(has_right & (origin <= chip))
        def _():
            line_copy(origin, m, True).wait_send()

        @pl.when(has_left & (origin >= chip))
        def _():
            line_copy(origin, m, False).wait_send()

        pair_copy(origin, m, core).wait_send()

        @pl.when((origin == 0) & has_next)
        def _():
            top_copy(m).wait_send()

        @pl.when((origin == 0) & has_prev)
        def _():
            bottom_copy(m).wait_send()

        return carry

    lax.fori_loop(0, chips * maps, drain, 0)


def per_device(vels, skies, psi_maps, phi_maps, psf_taps, shifts):
    frames, share, width = psi_maps.shape
    maps = 2 * frames
    tiles = width // LANES
    rows = share * vels
    trials = shifts.shape[0]
    dma = pltpu.SemaphoreType.DMA
    blurred, done = pl.pallas_call(
        functools.partial(gather_kernel, vels, skies),
        out_shape=(
            jax.ShapeDtypeStruct((maps, tiles + 1, rows + 2 * SHIFT, LANES), jnp.float32),
            jax.ShapeDtypeStruct((trials, rows, width), jnp.float32),
        ),
        in_specs=[
            pl.BlockSpec(memory_space=pltpu.SMEM),
            pl.BlockSpec(memory_space=pltpu.SMEM),
            pl.BlockSpec(memory_space=pl.ANY),
            pl.BlockSpec(memory_space=pl.ANY),
        ],
        out_specs=(pl.BlockSpec(memory_space=pltpu.VMEM), pl.BlockSpec(memory_space=pltpu.VMEM)),
        scratch_shapes=[
            pltpu.VMEM((vels, maps, share, width), jnp.float32),
            pltpu.VMEM((maps, tiles + 1, rows + 2 * EDGE, LANES), jnp.float32),
            pltpu.VMEM((maps, EDGE, width), jnp.float32),
            pltpu.VMEM((maps, EDGE, width), jnp.float32),
            pltpu.VMEM((2, 2, 2, 3 * LANES, LANES), jnp.bfloat16),
            pltpu.VMEM((2, psf_taps.shape[0], 8, LANES), jnp.float32),
            dma((2,)),
            dma((vels, maps)),
            dma((vels // 2, maps)),
            dma((vels // 2, maps)),
            dma((vels // 2, maps)),
            dma((maps,)),
            dma((maps,)),
            dma((maps,)),
            dma((maps,)),
        ],
        compiler_params=pltpu.CompilerParams(
            collective_id=0, has_side_effects=True, vmem_limit_bytes=24 * 2**20
        ),
        name="gather",
    )(psf_taps, shifts, psi_maps, phi_maps)
    return pl.pallas_call(
        functools.partial(stack_kernel, vels),
        out_shape=jax.ShapeDtypeStruct((trials, rows, width), jnp.float32),
        in_specs=[
            pl.BlockSpec(memory_space=pltpu.SMEM),
            pl.BlockSpec(memory_space=pltpu.VMEM),
            pl.BlockSpec(memory_space=pltpu.VMEM),
        ],
        out_specs=pl.BlockSpec(memory_space=pl.ANY),
        scratch_shapes=[
            pltpu.VMEM((trials, EDGE, width), jnp.float32),
            pltpu.VMEM((trials, 2 * share + EDGE, width), jnp.float32),
            dma((3, trials)),
        ],
        compiler_params=pltpu.CompilerParams(vmem_limit_bytes=4 * 2**20),
        name="stack",
    )(shifts, blurred, done)


def solution(mesh):
    return jax.shard_map(
        functools.partial(per_device, mesh.shape["vel"], mesh.shape["sky"]),
        mesh=mesh,
        in_specs=(
            P(None, ("sky", "vel"), None),
            P(None, ("sky", "vel"), None),
            P(),
            P("vel", None, None),
        ),
        out_specs=P("vel", "sky", None),
        check_vma=False,
    )
```

```python
import functools
import jax
import jax.numpy as jnp
from jax import lax
from jax.experimental import pallas as pl
from jax.experimental.pallas import tpu as pltpu
from jax.sharding import PartitionSpec as P

SHIFT = 16
EDGE = 24
LANES = 128
MESH = pl.DeviceIdType.MESH


def stack_rows(shifts_ref, maps_ref, out_ref, trial, first, count, shift, unroll):
    frames = shifts_ref.shape[1]
    tiles = maps_ref.shape[1]
    lane = lax.broadcasted_iota(jnp.int32, (8, LANES), 1)
    down, turn, inside = [], [], []
    for frame in range(1, frames):
        offset = shifts_ref[trial, frame, 1] + SHIFT
        down.append(shifts_ref[trial, frame, 0] + SHIFT)
        turn.append(lax.rem(LANES - offset, LANES))
        inside.append(lane >= offset)

    def one_group(group, carry):
        base = first + group * 8

        def stacked(kind):
            total = [
                maps_ref[kind * frames, tile, pl.ds(pl.multiple_of(base + SHIFT, 8), 8)]
                for tile in range(tiles - 1)
            ]
            for step in range(frames - 1):
                m = kind * frames + step + 1
                pieces = [maps_ref[m, tile, pl.ds(base + down[step], 8)] for tile in range(tiles)]
                for tile in range(tiles - 1):
                    joined = jnp.where(inside[step], pieces[tile], pieces[tile + 1])
                    total[tile] = total[tile] + pltpu.roll(joined, turn[step], 1)
            return total

        psi = stacked(0)
        phi = stacked(1)
        for tile in range(tiles - 1):
            out_ref[
                trial, pl.ds(pl.multiple_of(base - shift, 8), 8), tile * LANES : (tile + 1) * LANES
            ] = psi[tile] * lax.rsqrt(phi[tile])
        return carry

    lax.fori_loop(0, count // 8, one_group, 0, unroll=unroll)


def stack_kernel(vels, shifts_ref, maps_ref, done_ref, out_ref, near, far, sems):
    trials, rows, _ = done_ref.shape
    both = 2 * (rows // vels)
    chip = lax.axis_index("vel") // 2
    low = (chip < vels // 4).astype(jnp.int32)
    middle = rows - both - 2 * EDGE
    middle_row = pl.multiple_of(EDGE + (1 - low) * both, 8)
    near_row = pl.multiple_of((1 - low) * (rows - EDGE), 8)
    far_row = pl.multiple_of(low * (rows - both - EDGE), 8)

    def middle_copy(trial):
        part = pl.ds(middle_row, middle)
        return pltpu.make_async_copy(done_ref.at[trial, part], out_ref.at[trial, part], sems.at[0, trial])

    def near_copy(trial):
        return pltpu.make_async_copy(
            near.at[trial], out_ref.at[trial, pl.ds(near_row, EDGE)], sems.at[1, trial]
        )

    def far_copy(trial):
        return pltpu.make_async_copy(
            far.at[trial], out_ref.at[trial, pl.ds(far_row, both + EDGE)], sems.at[2, trial]
        )

    def begin(trial, carry):
        middle_copy(trial).start()
        return carry

    lax.fori_loop(0, trials, begin, 0)

    def compute(trial, carry):
        stack_rows(shifts_ref, maps_ref, near, trial, near_row, EDGE, near_row, 3)
        near_copy(trial).start()
        stack_rows(shifts_ref, maps_ref, far, trial, far_row, both + EDGE, far_row, True)
        far_copy(trial).start()
        return carry

    lax.fori_loop(0, trials, compute, 0)

    def finish(trial, carry):
        middle_copy(trial).wait()
        near_copy(trial).wait()
        far_copy(trial).wait()
        return carry

    lax.fori_loop(0, trials, finish, 0)


def gather_kernel(
    vels, skies, taps_ref, shifts_ref, psi_ref, phi_ref, out_ref, done_ref,
    raw, along, top, bottom, band, weight,
    own_sem, recv_sem, right_sem, left_sem, pair_sem, top_recv, bottom_recv, top_send, bottom_send,
):
    frames, share, width = psi_ref.shape
    taps = taps_ref.shape[0]
    half = taps // 2
    maps = 2 * frames
    chips = vels // 2
    tiles = width // LANES
    both = 2 * share
    rows = vels * share
    sky = lax.axis_index("sky")
    vel = lax.axis_index("vel")
    chip = vel // 2
    core = vel % 2
    has_right = chip < chips - 1
    has_left = chip > 0
    has_next = sky < skies - 1
    has_prev = sky > 0

    own_psi = pltpu.make_async_copy(psi_ref, raw.at[vel, pl.ds(0, frames)], own_sem.at[0])
    own_phi = pltpu.make_async_copy(phi_ref, raw.at[vel, pl.ds(frames, frames)], own_sem.at[1])
    own_psi.start()
    own_phi.start()

    neighbours = (
        (has_right, (sky, vel + 2)),
        (has_left, (sky, vel - 2)),
        (has_next, (sky + 1, vel)),
        (has_prev, (sky - 1, vel)),
    )
    partner = (sky, vel + 1 - 2 * core)
    barrier = pltpu.get_barrier_semaphore()
    pl.semaphore_signal(barrier, inc=1, device_id=partner, device_id_type=MESH)
    for present, device in neighbours:

        @pl.when(present)
        def _(device=device):
            pl.semaphore_signal(barrier, inc=1, device_id=device, device_id_type=MESH)

    peers = 1
    for present, _ in neighbours:
        peers = peers + present.astype(jnp.int32)
    pl.semaphore_wait(barrier, peers)
    def line_copy(origin, m, to_right):
        chunk = 2 * origin + core
        return pltpu.make_async_remote_copy(
            src_ref=raw.at[chunk, m],
            dst_ref=raw.at[chunk, m],
            send_sem=(right_sem if to_right else left_sem).at[origin, m],
            recv_sem=recv_sem.at[chunk, m],
            device_id=(sky, vel + 2) if to_right else (sky, vel - 2),
            device_id_type=MESH,
        )

    def pair_copy(origin, m, side):
        chunk = 2 * origin + side
        return pltpu.make_async_remote_copy(
            src_ref=raw.at[chunk, m],
            dst_ref=raw.at[chunk, m],
            send_sem=pair_sem.at[origin, m],
            recv_sem=recv_sem.at[chunk, m],
            device_id=partner,
            device_id_type=MESH,
        )

    def top_copy(m):
        return pltpu.make_async_remote_copy(
            src_ref=raw.at[vels - 1, m, pl.ds(share - EDGE, EDGE)],
            dst_ref=top.at[m],
            send_sem=top_send.at[m],
            recv_sem=top_recv.at[m],
            device_id=(sky + 1, vel),
            device_id_type=MESH,
        )

    def bottom_copy(m):
        return pltpu.make_async_remote_copy(
            src_ref=raw.at[0, m, pl.ds(0, EDGE)],
            dst_ref=bottom.at[m],
            send_sem=bottom_send.at[m],
            recv_sem=bottom_recv.at[m],
            device_id=(sky - 1, vel),
            device_id_type=MESH,
        )

    def send_own(m, carry):
        @pl.when(has_right)
        def _():
            line_copy(chip, m, True).start()

        @pl.when(has_left)
        def _():
            line_copy(chip, m, False).start()

        pair_copy(chip, m, core).start()
        return carry

    own_psi.wait()
    lax.fori_loop(0, frames, send_own, 0)
    own_phi.wait()
    lax.fori_loop(frames, maps, send_own, 0)

    total = taps_ref[0]
    for i in range(1, taps):
        total = total + taps_ref[i]
    scale = 1.0 / jnp.full((8, LANES), total, jnp.float32)
    for i in range(taps):
        value = jnp.full((8, LANES), taps_ref[i], jnp.float32) * scale
        weight[0, i] = value
        weight[1, i] = value * value
    place = lax.broadcasted_iota(jnp.int32, (3 * LANES, LANES), 0)
    place = place - lax.broadcasted_iota(jnp.int32, (3 * LANES, LANES), 1)
    for lead in range(2):
        spot = place - (LANES - SHIFT * lead - half)
        for kind in range(2):
            matrix = jnp.zeros((3 * LANES, LANES), jnp.float32)
            for i in range(taps):
                value = jnp.broadcast_to(weight[kind, i][:1], (3 * LANES, LANES))
                matrix = jnp.where(spot == i, value, matrix)
            coarse = matrix.astype(jnp.bfloat16)
            band[lead, kind, 0] = coarse
            band[lead, kind, 1] = (matrix - coarse.astype(jnp.float32)).astype(jnp.bfloat16)

    def blur_along(block, m, start):
        kind = m // frames
        count = block.shape[0]
        coarse = block.astype(jnp.bfloat16)
        fine = (block - coarse.astype(jnp.float32)).astype(jnp.bfloat16)

        def place_tiles(lead):
            for tile in range(tiles + lead):
                first, last = max(tile - 1, 0), min(tile + 2 - lead, tiles)
                columns = slice(first * LANES, last * LANES)
                offset = (first - tile + 1) * LANES
                depth = (last - first) * LANES
                high = band[lead, kind, 0, offset : offset + depth]
                low = band[lead, kind, 1, offset : offset + depth]
                value = jnp.dot(coarse[:, columns], high, preferred_element_type=jnp.float32)
                value += jnp.dot(fine[:, columns], high, preferred_element_type=jnp.float32)
                value += jnp.dot(coarse[:, columns], low, preferred_element_type=jnp.float32)
                if lead and tile in (0, tiles):
                    lane = lax.broadcasted_iota(jnp.int32, (count, LANES), 1)
                    value = jnp.where(lane >= SHIFT if tile == 0 else lane < SHIFT, value, 0.0)
                along[m, tile, pl.ds(start, count)] = value

        @pl.when(m % frames == 0)
        def _():
            place_tiles(0)

        @pl.when(m % frames > 0)
        def _():
            place_tiles(1)

    def blur_across(m, start, count):
        kind = m // frames
        factors = [weight[kind, i] for i in range(taps)]

        def one_tile(tile, carry):
            for group in range(count // 8):
                base = start + 8 * group
                value = factors[0] * along[m, tile, pl.ds(base + 8 - half, 8)]
                for i in range(1, taps):
                    value += factors[i] * along[m, tile, pl.ds(base + 8 - half + i, 8)]
                out_ref[m, tile, pl.ds(pl.multiple_of(base, 8), 8)] = value
            return carry

        lax.fori_loop(0, tiles + jnp.minimum(m % frames, 1), one_tile, 0)

    def arrive(distance, m):
        left = chip - distance
        right = chip + distance

        @pl.when((distance > 0) & (left >= 0))
        def _():
            line_copy(left, m, True).wait_recv()

            @pl.when(has_right)
            def _():
                line_copy(left, m, True).start()

            pair_copy(left, m, core).start()

        @pl.when((distance > 0) & (right < chips))
        def _():
            line_copy(right, m, False).wait_recv()

            @pl.when(has_left)
            def _():
                line_copy(right, m, False).start()

            pair_copy(right, m, core).start()

    def process(distance, m):
        def one_side(side, carry):
            origin = chip + (2 * side - 1) * distance

            @pl.when((origin >= 0) & (origin < chips) & ((side == 0) | (distance > 0)))
            def _():
                pair_copy(origin, m, 1 - core).wait_recv()

                @pl.when((origin == chips - 1) & has_next)
                def _():
                    top_copy(m).start()

                @pl.when((origin == 0) & has_prev)
                def _():
                    bottom_copy(m).start()

                def one_chunk(chunk, carry):
                    start = pl.multiple_of(EDGE + chunk * share, 8)
                    blur_along(raw[chunk, m], m, start)
                    return carry

                lax.fori_loop(2 * origin, 2 * origin + 2, one_chunk, 0)

                @pl.when(distance == 0)
                def _():
                    blur_across(m, SHIFT + origin * both + 8, both - 16)

                @pl.when(distance > 0)
                def _():
                    blur_across(m, SHIFT + origin * both + 8 - 16 * side, both)

            return carry

        lax.fori_loop(0, 2, one_side, 0)

    lead = jnp.where(chip < chips // 2, chips - 1, 0)

    def stack_side(distance, trial):
        def one_side(side, carry):
            origin = chip + (2 * side - 1) * distance
            wanted = (origin >= 0) & (origin < chips) & (origin != lead)

            @pl.when(wanted & (distance == 0) & (side == 0))
            def _():
                first = origin * both + EDGE
                stack_rows(shifts_ref, out_ref, done_ref, trial, first, both - 2 * EDGE, 0, 2)

            @pl.when(wanted & (distance > 0))
            def _():
                first = origin * both + EDGE - 2 * EDGE * side
                stack_rows(shifts_ref, out_ref, done_ref, trial, first, both, 0, 8)

            return carry

        lax.fori_loop(0, 2, one_side, 0)

    def step(index, carry):
        @pl.when(index < chips * maps)
        def _():
            arrive(index // maps, index % maps)

        @pl.when(index > 0)
        def _():
            process((index - 1) // maps, (index - 1) % maps)

        @pl.when(index > maps)
        def _():
            for block in range(0, shifts_ref.shape[0], maps):
                trial = (index - 1) % maps + block

                @pl.when(trial < shifts_ref.shape[0])
                def _(trial=trial):
                    stack_side((index - 1) // maps - 1, trial)

        return carry

    lax.fori_loop(0, chips * maps + 1, step, 0)

    def finish(m, carry):
        @pl.when(has_prev)
        def _():
            pltpu.make_async_copy(top.at[m], top.at[m], top_recv.at[m]).wait()
            blur_along(top[m], m, 0)
            blur_across(m, 0, EDGE)

        @pl.when(jnp.logical_not(has_prev))
        def _():
            for tile in range(tiles + 1):
                along[m, tile, pl.ds(0, EDGE)] = jnp.zeros((EDGE, LANES), jnp.float32)
            blur_across(m, SHIFT, 8)
            for tile in range(tiles + 1):
                out_ref[m, tile, pl.ds(0, SHIFT)] = jnp.zeros((SHIFT, LANES), jnp.float32)

        @pl.when(has_next)
        def _():
            pltpu.make_async_copy(bottom.at[m], bottom.at[m], bottom_recv.at[m]).wait()
            blur_along(bottom[m], m, EDGE + rows)
            blur_across(m, SHIFT + rows - 8, EDGE)

        @pl.when(jnp.logical_not(has_next))
        def _():
            for tile in range(tiles + 1):
                along[m, tile, pl.ds(EDGE + rows, EDGE)] = jnp.zeros((EDGE, LANES), jnp.float32)
            blur_across(m, SHIFT + rows - 8, 8)
            for tile in range(tiles + 1):
                out_ref[m, tile, pl.ds(SHIFT + rows, SHIFT)] = jnp.zeros((SHIFT, LANES), jnp.float32)

        return carry

    lax.fori_loop(0, maps, finish, 0)

    def drain(index, carry):
        origin = index // maps
        m = index % maps

        @pl.when(has_right & (origin <= chip))
        def _():
            line_copy(origin, m, True).wait_send()

        @pl.when(has_left & (origin >= chip))
        def _():
            line_copy(origin, m, False).wait_send()

        pair_copy(origin, m, core).wait_send()

        @pl.when((origin == 0) & has_next)
        def _():
            top_copy(m).wait_send()

        @pl.when((origin == 0) & has_prev)
        def _():
            bottom_copy(m).wait_send()

        return carry

    lax.fori_loop(0, chips * maps, drain, 0)


def per_device(vels, skies, psi_maps, phi_maps, psf_taps, shifts):
    frames, share, width = psi_maps.shape
    maps = 2 * frames
    tiles = width // LANES
    rows = share * vels
    trials = shifts.shape[0]
    dma = pltpu.SemaphoreType.DMA
    blurred, done = pl.pallas_call(
        functools.partial(gather_kernel, vels, skies),
        out_shape=(
            jax.ShapeDtypeStruct((maps, tiles + 1, rows + 2 * SHIFT, LANES), jnp.float32),
            jax.ShapeDtypeStruct((trials, rows, width), jnp.float32),
        ),
        in_specs=[
            pl.BlockSpec(memory_space=pltpu.SMEM),
            pl.BlockSpec(memory_space=pltpu.SMEM),
            pl.BlockSpec(memory_space=pl.ANY),
            pl.BlockSpec(memory_space=pl.ANY),
        ],
        out_specs=(pl.BlockSpec(memory_space=pltpu.VMEM), pl.BlockSpec(memory_space=pltpu.VMEM)),
        scratch_shapes=[
            pltpu.VMEM((vels, maps, share, width), jnp.float32),
            pltpu.VMEM((maps, tiles + 1, rows + 2 * EDGE, LANES), jnp.float32),
            pltpu.VMEM((maps, EDGE, width), jnp.float32),
            pltpu.VMEM((maps, EDGE, width), jnp.float32),
            pltpu.VMEM((2, 2, 2, 3 * LANES, LANES), jnp.bfloat16),
            pltpu.VMEM((2, psf_taps.shape[0], 8, LANES), jnp.float32),
            dma((2,)),
            dma((vels, maps)),
            dma((vels // 2, maps)),
            dma((vels // 2, maps)),
            dma((vels // 2, maps)),
            dma((maps,)),
            dma((maps,)),
            dma((maps,)),
            dma((maps,)),
        ],
        compiler_params=pltpu.CompilerParams(
            collective_id=0, has_side_effects=True, vmem_limit_bytes=24 * 2**20
        ),
        name="gather",
    )(psf_taps, shifts, psi_maps, phi_maps)
    return pl.pallas_call(
        functools.partial(stack_kernel, vels),
        out_shape=jax.ShapeDtypeStruct((trials, rows, width), jnp.float32),
        in_specs=[
            pl.BlockSpec(memory_space=pltpu.SMEM),
            pl.BlockSpec(memory_space=pltpu.VMEM),
            pl.BlockSpec(memory_space=pltpu.VMEM),
        ],
        out_specs=pl.BlockSpec(memory_space=pl.ANY),
        scratch_shapes=[
            pltpu.VMEM((trials, EDGE, width), jnp.float32),
            pltpu.VMEM((trials, 2 * share + EDGE, width), jnp.float32),
            dma((3, trials)),
        ],
        compiler_params=pltpu.CompilerParams(vmem_limit_bytes=4 * 2**20),
        name="stack",
    )(shifts, blurred, done)


def solution(mesh):
    return jax.shard_map(
        functools.partial(per_device, mesh.shape["vel"], mesh.shape["sky"]),
        mesh=mesh,
        in_specs=(
            P(None, ("sky", "vel"), None),
            P(None, ("sky", "vel"), None),
            P(),
            P("vel", None, None),
        ),
        out_specs=P("vel", "sky", None),
        check_vma=False,
    )
```
